32 devices in a mesh: pairs: 2 (over y), col: 4 (over z), row: 4 (over x, core).
Axes of the slice: x: 2, y: 2, z: 4, core: 2. Of those that a mesh axis runs over, the one named last changes fastest.
Arguments:
- images: float32 [4, 8, 64, 512], P('pairs', None, 'row', 'col'), parts along dimension 0, may hold values from -12 to 12
- conv_weight: bfloat16 [32, 72], replicated, may hold values from -0.75 to 0.75
- conv_bias: float32 [32], replicated, may hold values from -2.5 to 2.5
- agg_weight: float32 [8, 27], replicated, may hold values from -3.2 to 3.2
Outputs:
- disparity: float32 [128, 512], P(('pairs', 'row'), 'col'), parts along dimension 0
The draws below stay inside these ranges and needn't reach their ends.
There are 2 independent parts, one for each index of `pairs`. The reference program is written for one: setup_inputs(seed, part) draws one part's arguments, and reference() takes and returns one part's arrays. A program takes and returns all parts, laid end to end along the dimension named above; an argument that names none is the same for every part. Nothing has to cross between parts.
All inputs are finite; a program needn't handle non-finite values.
Results may differ from the reference program's by a relative error of at most 0.012.
The reference program's roundings to bfloat16 on the way count: a program that leaves them out, or rounds other values in their place, can miss the bound.
Values may be sent and summed in bfloat16 or wider, within the bound.
A program may use at most 64 MiB of HBM per device.

```python
import jax
import jax.numpy as jnp
from jax import lax

CIN = 8
F = 32
G = 8
D = 64
DB = 16
H = 64
W = 512


def draw_images(key, part):
    values = jax.random.normal(key, (2, CIN, H, W), jnp.float32)
    return jnp.clip(values, -12.0, 12.0)


def centred(key, shape, deviation, most, kind=jnp.bfloat16):
    array = jax.random.normal(key, shape, jnp.float32) * deviation
    return jnp.minimum(jnp.maximum(array, -most), most).astype(kind)


def setup_inputs(seed: int = 0, part: int = 0) -> dict:
    seeds = jax.random.split(jax.random.key(seed), 5)
    own_keys = jax.random.split(jax.random.fold_in(seeds[4], part), 5)
    images = draw_images(jax.random.fold_in(jax.random.fold_in(seeds[4], part), 71), part)
    conv_weight = centred(seeds[1], (F, 9 * CIN), (9 * CIN) ** -0.5, 0.75)
    conv_bias = centred(seeds[2], (F,), 0.5, 2.5, jnp.float32)
    agg_weight = centred(seeds[3], (G, 27), 0.8, 3.2, jnp.float32)
    return {"images": images, "conv_weight": conv_weight, "conv_bias": conv_bias, "agg_weight": agg_weight}


def conv_valid(picture, conv_weight, conv_bias):
    height = picture.shape[1] - 2
    width_out = picture.shape[2] - 2
    patches = jnp.concatenate([picture[:, step_y:step_y + height, step_x:step_x + width_out] for step_y in range(3) for step_x in range(3)], axis=0)
    flattened = patches.reshape(patches.shape[0], height * width_out)
    summed = jnp.dot(conv_weight, flattened, preferred_element_type=jnp.float32) + conv_bias[:, None]
    return jax.nn.leaky_relu(summed, 0.1).reshape(conv_weight.shape[0], height, width_out)


def block_costs(left_feat, right_full, start_d, search, block_depth, groups):
    channels, height, width_out = left_feat.shape
    window = lax.dynamic_slice_in_dim(right_full, search - start_d - block_depth, width_out + block_depth + 1, 2)
    left_grouped = left_feat.reshape(groups, channels // groups, height, width_out)
    layers = []
    for offset in range(block_depth + 2):
        shifted = window[:, :, block_depth + 1 - offset:block_depth + 1 - offset + width_out]
        product = jnp.einsum("gcyx,gcyx->gyx", left_grouped, shifted.reshape(groups, channels // groups, height, width_out), preferred_element_type=jnp.float32) * (groups / channels)
        disparity = start_d - 1 + offset
        usable = jnp.logical_and(disparity >= 0, disparity < search).astype(jnp.float32)
        layers.append((product * usable).astype(jnp.bfloat16))
    return jnp.stack(layers, axis=1)


def aggregate(cost_block, agg_weight, block_depth, height, width_out):
    tapped = jnp.einsum("gdyx,gk->kdyx", cost_block.astype(jnp.float32), agg_weight, precision=lax.Precision.HIGHEST)
    summed = jnp.zeros((block_depth, height, width_out), jnp.float32)
    for step_d in range(3):
        for step_y in range(3):
            for step_x in range(3):
                summed = summed + tapped[9 * step_d + 3 * step_y + step_x, step_d:step_d + block_depth, step_y:step_y + height, step_x:step_x + width_out]
    return summed


def softmax_update(running, scores, start_d):
    running_max, running_sum, running_moment = running
    values = (start_d + lax.iota(jnp.int32, scores.shape[0])).astype(jnp.float32)
    new_max = jnp.maximum(running_max, jnp.max(scores, axis=0))
    rescale = jnp.exp(running_max - new_max)
    weights = jnp.exp(scores - new_max[None])
    return (new_max, running_sum * rescale + jnp.sum(weights, axis=0), running_moment * rescale + jnp.sum(weights * values[:, None, None], axis=0))


def reference(images, conv_weight, conv_bias, agg_weight):
    pictures = images.astype(jnp.bfloat16)
    padded = jnp.pad(pictures, ((0, 0), (0, 0), (1, 1), (1, 1)))
    left_feat = conv_valid(padded[0], conv_weight, conv_bias).astype(jnp.bfloat16)
    right_feat = conv_valid(padded[1], conv_weight, conv_bias).astype(jnp.bfloat16)
    channels = left_feat.shape[0]
    right_full = jnp.concatenate([jnp.zeros((channels, H, D), jnp.bfloat16), right_feat, jnp.zeros((channels, H, 1), jnp.bfloat16)], axis=2)

    def advance(running, block_index):
        start_d = block_index * DB
        cost_block = block_costs(left_feat, right_full, start_d, D, DB, G)
        cost_block = jnp.pad(cost_block, ((0, 0), (0, 0), (1, 1), (1, 1)))
        scores = aggregate(cost_block, agg_weight, DB, H, W)
        return softmax_update(running, scores, start_d), None

    initial = (jnp.full((H, W), -1e30, jnp.float32), jnp.zeros((H, W), jnp.float32), jnp.zeros((H, W), jnp.float32))
    running, unused = lax.scan(advance, initial, jnp.arange(D // DB, dtype=jnp.int32))
    return running[2] / running[1] / D
```

```python
import functools

import jax
import jax.numpy as jnp
from jax import lax
from jax.experimental import pallas as pl
from jax.experimental.pallas import tpu as pltpu
from jax.sharding import PartitionSpec as P

D = 64
BAND = 4


def shifted(shard, axes, sizes, steps):
    pairs = []
    for r in range(sizes[1]):
        for c in range(sizes[0]):
            to_r, to_c = r - steps[0], c - steps[1]
            if 0 <= to_r < sizes[1] and 0 <= to_c < sizes[0]:
                pairs.append((c * sizes[1] + r, to_c * sizes[1] + to_r))
    return lax.ppermute(shard, axes, pairs)


def body(shape, pt_ref, q_ref, bias_ref, agg_ref, out_ref, wc, amat, lf, rf, cost, acc, score):
    rows, cols, groups, per, cin = shape
    lanes = wc.shape[2] // per
    lead = D + 8
    span = rf.shape[1]
    tiles = lanes // 128
    total_rows = rows * lax.axis_size("row")
    total_cols = cols * lax.axis_size("col")
    top = lax.axis_index("row") * rows - 1
    left = lax.axis_index("col") * cols

    lane_row = lax.broadcasted_iota(jnp.int32, (cin, lanes), 1) // groups
    for step_x in range(3):
        for ch in range(per):
            taps = []
            for step_y in range(3):
                base = ((step_y * 3 + step_x) * per + ch) * cin
                taps.append(q_ref[base : base + cin, :])
            for pair in range((rows + 4) // 2):
                halves = []
                for line in (2 * pair, 2 * pair + 1):
                    value = jnp.zeros((cin, lanes), jnp.float32)
                    for step_y in range(3):
                        value = jnp.where(lane_row == line - step_y, taps[step_y], value)
                    halves.append(value)
                wc[step_x, pair * 2 * cin : (pair + 1) * 2 * cin, ch * lanes : (ch + 1) * lanes] = (
                    jnp.concatenate(halves, axis=0).astype(jnp.bfloat16)
                )
    used = (rows + 4) * cin
    if used < lanes:
        wc[:, used:, :] = jnp.zeros((3, lanes - used, per * lanes), jnp.bfloat16)

    off = (
        lax.broadcasted_iota(jnp.int32, (rows, lanes), 1) // groups
        - lax.broadcasted_iota(jnp.int32, (rows, lanes), 0)
    )
    for step_d in range(3):
        for step_x in range(3):
            value = jnp.zeros((rows, lanes), jnp.float32)
            for step_y in range(3):
                k = 9 * step_d + 3 * step_y + step_x
                value = jnp.where(off == step_y, agg_ref[k : k + 1, :], value)
            high = value.astype(jnp.bfloat16)
            low = (value - high.astype(jnp.float32)).astype(jnp.bfloat16)
            at = (step_d * 3 + step_x) * 2 * rows
            amat[at : at + rows, :] = high
            amat[at + rows : at + 2 * rows, :] = low

    def features(image, first, count, store, scale):
        row_ids = left + first - lead + lax.broadcasted_iota(jnp.int32, (count, lanes), 0)
        line = top + lax.broadcasted_iota(jnp.int32, (count, lanes), 1) // groups
        keep = (row_ids >= 0) & (row_ids < total_cols) & (line >= 0) & (line < total_rows)
        parts = [
            pt_ref[image, 7 + step_x + first : 7 + step_x + first + count, :].astype(jnp.bfloat16)
            for step_x in range(3)
        ]
        for ch in range(per):
            summed = jnp.broadcast_to(bias_ref[ch : ch + 1, :], (count, lanes))
            total = None
            for step_x in range(3):
                term = jnp.dot(
                    parts[step_x],
                    wc[step_x, :, ch * lanes : (ch + 1) * lanes],
                    preferred_element_type=jnp.float32,
                )
                total = term if total is None else total + term
            summed = total + summed
            feat = jnp.where(summed >= 0, summed, summed * 0.1)
            feat = feat.astype(jnp.bfloat16).astype(jnp.float32)
            feat = jnp.where(keep, feat * scale, 0.0)
            for tile in range(tiles):
                store[ch * tiles + tile, :, :] = feat[:, tile * 128 : (tile + 1) * 128]

    features(0, lead - 8, cols + 16, lf, 1.0 / per)
    features(1, 0, span, rf, 1.0)

    for tile in range(tiles):
        for chunk in range(cols // 16):
            lefts = [
                lf[ch * tiles + tile, 8 + chunk * 16 : 24 + chunk * 16, :] for ch in range(per)
            ]

            def layer(d, carry):
                total = None
                for ch in range(per):
                    term = (
                        lefts[ch] * rf[ch * tiles + tile, pl.ds(lead + chunk * 16 - d, 16), :]
                    )
                    total = term if total is None else total + term
                cost[d, chunk * 16 : (chunk + 1) * 16, tile * 128 : (tile + 1) * 128] = (
                    total.astype(jnp.bfloat16)
                )
                return carry

            lax.fori_loop(0, D, layer, 0, unroll=4)

    edges = []
    for at, begin in ((7, lead - D), (8 + cols, lead + cols - D + 1)):
        parts = []
        for tile in range(tiles):
            total = None
            for ch in range(per):
                k = ch * tiles + tile
                term = lf[k, at : at + 1, :] * rf[k, begin : begin + D, :]
                total = term if total is None else total + term
            parts.append(total.astype(jnp.bfloat16))
        edges.append(jnp.concatenate(parts, axis=1))
    edge = jnp.concatenate(edges, axis=0)
    nt = (((1,), (1,)), ((), ()))
    side = lax.dot_general(amat[...], edge, nt, preferred_element_type=jnp.float32)
    place = lax.broadcasted_iota(jnp.int32, (rows, 2 * D), 1)
    within = jnp.where(place >= D, place - D, place)
    border = None
    for step_d in range(3):
        pick = []
        for step_x in (0, 2):
            at = (step_d * 3 + step_x) * 2 * rows
            pick.append(side[at : at + rows, :] + side[at + rows : at + 2 * rows, :])
        value = jnp.where(place < D, pick[0], pick[1])
        if step_d == 0:
            value = jnp.where(within == D - 1, 0.0, pltpu.roll(value, 2 * D - 1, 1))
        elif step_d == 2:
            value = jnp.where(within == 0, 0.0, pltpu.roll(value, 1, 1))
        border = value if border is None else border + value

    acc[...] = jnp.zeros_like(acc)

    def band(block, carry):
        d0 = block * BAND
        stack = cost[pl.ds(d0, BAND), :, :].reshape(BAND * cols, lanes)
        got = lax.dot_general(amat[...], stack, nt, preferred_element_type=jnp.float32)
        for step_x in range(3):
            for o in range(BAND + 2):
                value = acc[step_x, d0 + o, :, :]
                for step_d in range(3):
                    j = o + step_d - 2
                    if 0 <= j < BAND:
                        at = (step_d * 3 + step_x) * 2 * rows
                        value += got[at : at + rows, j * cols : (j + 1) * cols]
                        value += got[at + rows : at + 2 * rows, j * cols : (j + 1) * cols]
                acc[step_x, d0 + o, :, :] = value
        return carry

    lax.fori_loop(0, D // BAND, band, 0)

    lane = lax.broadcasted_iota(jnp.int32, (rows, cols), 1)

    def finish(d, best):
        before = jnp.where(
            lane == 0,
            pltpu.roll(border, lax.rem(d + D + 1, 2 * D), 1),
            pltpu.roll(acc[0, d + 1, :, :], 1, 1),
        )
        after = jnp.where(
            lane == cols - 1, pltpu.roll(border, d, 1), pltpu.roll(acc[2, d + 1, :, :], cols - 1, 1)
        )
        value = acc[1, d + 1, :, :] + before + after
        score[d, :, :] = value
        return jnp.maximum(best, value)

    best = lax.fori_loop(0, D, finish, jnp.full((rows, cols), -jnp.inf, jnp.float32), unroll=4)

    def weigh(d, carry):
        total, moment = carry
        weight = jnp.exp(score[d, :, :] - best)
        return total + weight, moment + weight * d.astype(jnp.float32)

    zero = jnp.zeros((rows, cols), jnp.float32)
    total, moment = lax.fori_loop(0, D, weigh, (zero, zero), unroll=4)
    out_ref[...] = moment / total / D


def on_device(images, conv_weight, conv_bias, agg_weight):
    cin, rows, cols = images.shape[1:]
    groups = agg_weight.shape[0]
    per = conv_weight.shape[0] // groups
    lanes = -(-max((rows + 2) * groups, (rows + 4) * cin) // 128) * 128
    span = cols + D + 16
    sizes = (lax.axis_size("col"), lax.axis_size("row"))
    pictures = images.astype(jnp.bfloat16)
    move = functools.partial(shifted, axes=("col", "row"), sizes=sizes)
    wide = D + 2
    grid = []
    for r, lines in ((-1, slice(rows - 2, rows)), (0, slice(0, rows)), (1, slice(0, 2))):
        line = []
        for c, columns in ((-1, slice(cols - wide, cols)), (0, slice(0, cols)), (1, slice(0, 2))):
            piece = pictures[:, :, lines, columns]
            line.append(piece if r == 0 and c == 0 else move(piece, steps=(r, c)))
        grid.append(jnp.concatenate(line, axis=3))
    ext = jnp.concatenate(grid, axis=2)
    pt = ext.transpose(0, 3, 2, 1).reshape(2, ext.shape[3], (rows + 4) * cin).astype(jnp.float32)
    ahead = 16 + D - wide
    pt = jnp.pad(
        pt, ((0, 0), (ahead, span + 16 - ahead - pt.shape[1]), (0, lanes - pt.shape[2]))
    )
    repeat = lanes // groups
    q = conv_weight.reshape(groups, per, 9, cin).transpose(2, 1, 3, 0).astype(jnp.float32)
    q = jnp.tile(q.reshape(9 * per * cin, groups), (1, repeat))
    bias = jnp.tile(conv_bias.reshape(groups, per).T, (1, repeat))
    agg = jnp.tile(agg_weight.T, (1, repeat))
    return pl.pallas_call(
        functools.partial(body, (rows, cols, groups, per, cin)),
        out_shape=jax.ShapeDtypeStruct((rows, cols), jnp.float32),
        in_specs=[pl.BlockSpec(memory_space=pltpu.VMEM)] * 4,
        out_specs=pl.BlockSpec(memory_space=pltpu.VMEM),
        scratch_shapes=[
            pltpu.VMEM((3, lanes, per * lanes), jnp.bfloat16),
            pltpu.VMEM((18 * rows, lanes), jnp.bfloat16),
            pltpu.VMEM((per * (lanes // 128), cols + 16, 128), jnp.float32),
            pltpu.VMEM((per * (lanes // 128), span, 128), jnp.float32),
            pltpu.VMEM((D, cols, lanes), jnp.bfloat16),
            pltpu.VMEM((3, D + 2, rows, cols), jnp.float32),
            pltpu.VMEM((D, rows, cols), jnp.float32),
        ],
    )(pt, q, bias, agg)


def solution(mesh):
    in_specs = (P("pairs", None, "row", "col"), P(), P(), P())
    out_specs = P(("pairs", "row"), "col")
    return jax.shard_map(
        on_device, mesh=mesh, in_specs=in_specs, out_specs=out_specs, check_vma=False
    )
```

```python
import functools

import jax
import jax.numpy as jnp
from jax import lax
from jax.experimental import pallas as pl
from jax.experimental.pallas import tpu as pltpu
from jax.sharding import PartitionSpec as P

D = 64
BAND = 4


MESH = pl.DeviceIdType.MESH
STEPS = ((0, 1), (0, -1), (1, 0), (-1, 0), (1, 1), (1, -1), (-1, 1), (-1, -1))


def body(
    shape, tr_ref, edge_ref, weight_ref, bias_in, agg_in, out_ref,
    pt, wc, amat, lf, rf, cost, acc, score, near0, near1, far, lines, send_sem, recv_sem,
):
    rows, cols, groups, per, cin = shape
    lanes = wc.shape[2] // per
    lead = D + 8
    span = rf.shape[1]
    tiles = lanes // 128
    rows_axis, cols_axis = lax.axis_size("row"), lax.axis_size("col")
    my_row, my_col = lax.axis_index("row"), lax.axis_index("col")
    total_rows = rows * rows_axis
    total_cols = cols * cols_axis
    top = my_row * rows - 1
    left = my_col * cols
    reach = near1.shape[0]

    def exists(step):
        r, c = my_row + step[0], my_col + step[1]
        return (r >= 0) & (r < rows_axis) & (c >= 0) & (c < cols_axis)

    def device(step):
        return {"row": my_row + step[0], "col": my_col + step[1]}

    barrier = pltpu.get_barrier_semaphore()
    for step in STEPS:

        @pl.when(exists(step))
        def _(step=step):
            pl.semaphore_signal(barrier, inc=1, device_id=device(step), device_id_type=MESH)

    tall = 1 + (my_row > 0).astype(jnp.int32) + (my_row < rows_axis - 1).astype(jnp.int32)
    wide = 1 + (my_col > 0).astype(jnp.int32) + (my_col < cols_axis - 1).astype(jnp.int32)
    pl.semaphore_wait(barrier, tall * wide - 1)

    plan = [
        ((0, 1), tr_ref.at[1, pl.ds(cols - reach, reach), :], near1),
        ((0, 1), tr_ref.at[0, pl.ds(cols - 16, 16), :], near0),
        ((0, -1), tr_ref.at[:, pl.ds(0, 16), :], far),
    ]
    for r in (1, -1):
        side = 0 if r == 1 else 1
        for c in (0, 1, -1):
            plan.append(((r, c), edge_ref.at[1 - side], lines.at[side, 1 - c]))
    copies = []
    for k, (step, source, target) in enumerate(plan):
        copy = pltpu.make_async_remote_copy(
            src_ref=source,
            dst_ref=target,
            send_sem=send_sem.at[k],
            recv_sem=recv_sem.at[k],
            device_id=device(step),
            device_id_type=MESH,
        )
        copies.append((step, copy))

        @pl.when(exists(step))
        def _(copy=copy):
            copy.start()

        @pl.when(jnp.logical_not(exists((-step[0], -step[1]))))
        def _(target=target):
            target[...] = jnp.zeros(target.shape, target.dtype)

    spread_at = lax.broadcasted_iota(jnp.int32, (groups * per, lanes), 1) % groups * per
    spread_from = lax.broadcasted_iota(jnp.int32, (groups * per, lanes), 0)
    tn = (((0,), (0,)), ((), ()))
    weight = weight_ref[...].astype(jnp.float32)
    q, bias = [], []
    for ch in range(per):
        spread = (spread_from == spread_at + ch).astype(jnp.float32)
        q.append(
            lax.dot_general(weight, spread, tn, preferred_element_type=jnp.float32)
        )
        bias.append(
            jnp.dot(
                bias_in[...], spread,
                precision=lax.Precision.HIGHEST, preferred_element_type=jnp.float32,
            )
        )
    one = (
        lax.broadcasted_iota(jnp.int32, (groups, lanes), 0)
        == lax.broadcasted_iota(jnp.int32, (groups, lanes), 1) % groups
    ).astype(jnp.float32)
    agg = lax.dot_general(
        agg_in[...], one, tn,
        precision=lax.Precision.HIGHEST, preferred_element_type=jnp.float32,
    )

    lane_row = lax.broadcasted_iota(jnp.int32, (cin, lanes), 1) // groups
    order = list(range(2, rows + 2)) + [0, 1, rows + 2, rows + 3]
    for step_x in range(3):
        for ch in range(per):
            taps = []
            for step_y in range(3):
                base = (step_y * 3 + step_x) * cin
                taps.append(q[ch][base : base + cin, :])
            for pair in range((rows + 4) // 2):
                halves = []
                for line in order[2 * pair : 2 * pair + 2]:
                    value = jnp.zeros((cin, lanes), jnp.float32)
                    for step_y in range(3):
                        value = jnp.where(lane_row == line - step_y, taps[step_y], value)
                    halves.append(value)
                wc[step_x, pair * 2 * cin : (pair + 1) * 2 * cin, ch * lanes : (ch + 1) * lanes] = (
                    jnp.concatenate(halves, axis=0).astype(jnp.bfloat16)
                )
    used = (rows + 4) * cin
    if used < lanes:
        wc[:, used:, :] = jnp.zeros((3, lanes - used, per * lanes), jnp.bfloat16)

    off = (
        lax.broadcasted_iota(jnp.int32, (rows, lanes), 1) // groups
        - lax.broadcasted_iota(jnp.int32, (rows, lanes), 0)
    )
    for step_d in range(3):
        for step_x in range(3):
            value = jnp.zeros((rows, lanes), jnp.float32)
            for step_y in range(3):
                k = 9 * step_d + 3 * step_y + step_x
                value = jnp.where(off == step_y, agg[k : k + 1, :], value)
            high = value.astype(jnp.bfloat16)
            low = (value - high.astype(jnp.float32)).astype(jnp.bfloat16)
            at = (step_d * 3 + step_x) * 2 * rows
            amat[at : at + rows, :] = high
            amat[at + rows : at + 2 * rows, :] = low

    for step, copy in copies:

        @pl.when(exists((-step[0], -step[1])))
        def _(copy=copy):
            copy.wait_recv()

    base = 16 + D
    main = rows * cin
    pt[1, base - reach : base, 0:main] = near1[...].astype(jnp.float32)
    pt[0, base - 16 : base, 0:main] = near0[...].astype(jnp.float32)
    pt[:, base : base + cols, 0:main] = tr_ref[...].astype(jnp.float32)
    pt[:, base + cols : base + cols + 16, 0:main] = far[...].astype(jnp.float32)
    half = 2 * cin
    for image in range(2):
        for place in range(3):
            block = jnp.concatenate(
                [
                    lines[side, place, image * half : (image + 1) * half, :].astype(jnp.float32)
                    for side in range(2)
                ]
                + [jnp.zeros((lanes - main - 2 * half, cols), jnp.float32)],
                axis=0,
            )
            block = block.T
            if place == 0:
                pt[image, base - reach : base, main:] = block[cols - reach :, :]
            elif place == 1:
                pt[image, base : base + cols, main:] = block
            else:
                pt[image, base + cols : base + cols + 16, main:] = block[:16, :]

    def features(image, first, count, store, scale):
        row_ids = left + first - lead + lax.broadcasted_iota(jnp.int32, (count, lanes), 0)
        line = top + lax.broadcasted_iota(jnp.int32, (count, lanes), 1) // groups
        keep = (row_ids >= 0) & (row_ids < total_cols) & (line >= 0) & (line < total_rows)
        parts = [
            pt[image, 7 + step_x + first : 7 + step_x + first + count, :].astype(jnp.bfloat16)
            for step_x in range(3)
        ]
        for ch in range(per):
            summed = jnp.broadcast_to(bias[ch], (count, lanes))
            total = None
            for step_x in range(3):
                term = jnp.dot(
                    parts[step_x],
                    wc[step_x, :, ch * lanes : (ch + 1) * lanes],
                    preferred_element_type=jnp.float32,
                )
                total = term if total is None else total + term
            summed = total + summed
            feat = jnp.where(summed >= 0, summed, summed * 0.1)
            feat = feat.astype(jnp.bfloat16).astype(jnp.float32)
            feat = jnp.where(keep, feat * scale, 0.0)
            for tile in range(tiles):
                store[ch * tiles + tile, :, :] = feat[:, tile * 128 : (tile + 1) * 128]

    features(0, lead - 8, cols + 16, lf, 1.0 / per)
    features(1, 0, span, rf, 1.0)

    for tile in range(tiles):
        for chunk in range(cols // 16):
            lefts = [
                lf[ch * tiles + tile, 8 + chunk * 16 : 24 + chunk * 16, :] for ch in range(per)
            ]

            def layer(d, carry):
                total = None
                for ch in range(per):
                    term = (
                        lefts[ch] * rf[ch * tiles + tile, pl.ds(lead + chunk * 16 - d, 16), :]
                    )
                    total = term if total is None else total + term
                cost[d, chunk * 16 : (chunk + 1) * 16, tile * 128 : (tile + 1) * 128] = (
                    total.astype(jnp.bfloat16)
                )
                return carry

            lax.fori_loop(0, D, layer, 0, unroll=4)

    edges = []
    for at, begin in ((7, lead - D), (8 + cols, lead + cols - D + 1)):
        parts = []
        for tile in range(tiles):
            total = None
            for ch in range(per):
                k = ch * tiles + tile
                term = lf[k, at : at + 1, :] * rf[k, begin : begin + D, :]
                total = term if total is None else total + term
            parts.append(total.astype(jnp.bfloat16))
        edges.append(jnp.concatenate(parts, axis=1))
    edge = jnp.concatenate(edges, axis=0)
    nt = (((1,), (1,)), ((), ()))
    side = lax.dot_general(amat[...], edge, nt, preferred_element_type=jnp.float32)
    place = lax.broadcasted_iota(jnp.int32, (rows, 2 * D), 1)
    within = jnp.where(place >= D, place - D, place)
    border = None
    for step_d in range(3):
        pick = []
        for step_x in (0, 2):
            at = (step_d * 3 + step_x) * 2 * rows
            pick.append(side[at : at + rows, :] + side[at + rows : at + 2 * rows, :])
        value = jnp.where(place < D, pick[0], pick[1])
        if step_d == 0:
            value = jnp.where(within == D - 1, 0.0, pltpu.roll(value, 2 * D - 1, 1))
        elif step_d == 2:
            value = jnp.where(within == 0, 0.0, pltpu.roll(value, 1, 1))
        border = value if border is None else border + value

    acc[...] = jnp.zeros_like(acc)

    def band(block, carry):
        d0 = block * BAND
        stack = cost[pl.ds(d0, BAND), :, :].reshape(BAND * cols, lanes)
        got = lax.dot_general(amat[...], stack, nt, preferred_element_type=jnp.float32)
        for step_x in range(3):
            for o in range(BAND + 2):
                value = acc[step_x, d0 + o, :, :]
                for step_d in range(3):
                    j = o + step_d - 2
                    if 0 <= j < BAND:
                        at = (step_d * 3 + step_x) * 2 * rows
                        value += got[at : at + rows, j * cols : (j + 1) * cols]
                        value += got[at + rows : at + 2 * rows, j * cols : (j + 1) * cols]
                acc[step_x, d0 + o, :, :] = value
        return carry

    lax.fori_loop(0, D // BAND, band, 0)

    lane = lax.broadcasted_iota(jnp.int32, (rows, cols), 1)

    def finish(d, best):
        before = jnp.where(
            lane == 0,
            pltpu.roll(border, lax.rem(d + D + 1, 2 * D), 1),
            pltpu.roll(acc[0, d + 1, :, :], 1, 1),
        )
        after = jnp.where(
            lane == cols - 1, pltpu.roll(border, d, 1), pltpu.roll(acc[2, d + 1, :, :], cols - 1, 1)
        )
        value = acc[1, d + 1, :, :] + before + after
        score[d, :, :] = value
        return jnp.maximum(best, value)

    best = lax.fori_loop(0, D, finish, jnp.full((rows, cols), -jnp.inf, jnp.float32), unroll=4)

    def weigh(d, carry):
        total, moment = carry
        weight = jnp.exp(score[d, :, :] - best)
        return total + weight, moment + weight * d.astype(jnp.float32)

    zero = jnp.zeros((rows, cols), jnp.float32)
    total, moment = lax.fori_loop(0, D, weigh, (zero, zero), unroll=4)
    out_ref[...] = moment / total / D

    for step, copy in copies:

        @pl.when(exists(step))
        def _(copy=copy):
            copy.wait_send()


def on_device(images, conv_weight, conv_bias, agg_weight):
    cin, rows, cols = images.shape[1:]
    groups = agg_weight.shape[0]
    per = conv_weight.shape[0] // groups
    main = rows * cin
    lanes = main + 128
    span = cols + D + 16
    reach = -(-(D + 2) // 16) * 16
    pictures = images.astype(jnp.bfloat16).transpose(0, 2, 1, 3)
    tr = pictures.reshape(2, main, cols).transpose(0, 2, 1)
    edges = jnp.stack([pictures[:, :2], pictures[:, rows - 2 :]]).reshape(2, 4 * cin, cols)
    return pl.pallas_call(
        functools.partial(body, (rows, cols, groups, per, cin)),
        out_shape=jax.ShapeDtypeStruct((rows, cols), jnp.float32),
        in_specs=[pl.BlockSpec(memory_space=pltpu.VMEM)] * 5,
        out_specs=pl.BlockSpec(memory_space=pltpu.VMEM),
        scratch_shapes=[
            pltpu.VMEM((2, span + 16, lanes), jnp.float32),
            pltpu.VMEM((3, lanes, per * lanes), jnp.bfloat16),
            pltpu.VMEM((18 * rows, lanes), jnp.bfloat16),
            pltpu.VMEM((per * (lanes // 128), cols + 16, 128), jnp.float32),
            pltpu.VMEM((per * (lanes // 128), span, 128), jnp.float32),
            pltpu.VMEM((D, cols, lanes), jnp.bfloat16),
            pltpu.VMEM((3, D + 2, rows, cols), jnp.float32),
            pltpu.VMEM((D, rows, cols), jnp.float32),
            pltpu.VMEM((16, main), jnp.bfloat16),
            pltpu.VMEM((reach, main), jnp.bfloat16),
            pltpu.VMEM((2, 16, main), jnp.bfloat16),
            pltpu.VMEM((2, 3, 4 * cin, cols), jnp.bfloat16),
            pltpu.SemaphoreType.DMA((9,)),
            pltpu.SemaphoreType.DMA((9,)),
        ],
        compiler_params=pltpu.CompilerParams(collective_id=0, has_side_effects=True),
    )(tr, edges, conv_weight, conv_bias[None], agg_weight)


def solution(mesh):
    in_specs = (P("pairs", None, "row", "col"), P(), P(), P())
    out_specs = P(("pairs", "row"), "col")
    return jax.shard_map(
        on_device, mesh=mesh, in_specs=in_specs, out_specs=out_specs, check_vma=False
    )
```

```python
import functools

import jax
import jax.numpy as jnp
from jax import lax
from jax.experimental import pallas as pl
from jax.experimental.pallas import tpu as pltpu
from jax.sharding import PartitionSpec as P

D = 64


MESH = pl.DeviceIdType.MESH
STEPS = ((0, 1), (0, -1), (1, 0), (-1, 0), (1, 1), (1, -1), (-1, 1), (-1, -1))


def body(
    shape, tr_ref, edge_ref, weight_ref, bias_in, agg_in, out_ref,
    pt, wc, amat, lf, rf, raw, cost, acc, score, near0, near1, far, lines, send_sem, recv_sem,
):
    rows, cols, groups, per, cin = shape
    lanes = wc.shape[2] // per
    lead = D + 8
    span = rf.shape[1]
    tiles = lanes // 128
    rows_axis, cols_axis = lax.axis_size("row"), lax.axis_size("col")
    my_row, my_col = lax.axis_index("row"), lax.axis_index("col")
    total_rows = rows * rows_axis
    total_cols = cols * cols_axis
    top = my_row * rows - 1
    left = my_col * cols
    reach = near1.shape[0]
    skew = 128 // (2 * groups)

    def row_of(lane):
        beside = jnp.where((lane // groups) % 2 == 0, 0, rows + 1)
        return jnp.where(lane < rows * groups, lane // groups + 1, beside)

    def skew_of(lane):
        return (lane - rows * groups) // (2 * groups)


    def exists(step):
        r, c = my_row + step[0], my_col + step[1]
        return (r >= 0) & (r < rows_axis) & (c >= 0) & (c < cols_axis)

    def device(step):
        return {"row": my_row + step[0], "col": my_col + step[1]}

    barrier = pltpu.get_barrier_semaphore()
    for step in STEPS:

        @pl.when(exists(step))
        def _(step=step):
            pl.semaphore_signal(barrier, inc=1, device_id=device(step), device_id_type=MESH)

    tall = 1 + (my_row > 0).astype(jnp.int32) + (my_row < rows_axis - 1).astype(jnp.int32)
    wide = 1 + (my_col > 0).astype(jnp.int32) + (my_col < cols_axis - 1).astype(jnp.int32)
    pl.semaphore_wait(barrier, tall * wide - 1)

    plan = [
        ((0, 1), tr_ref.at[1, pl.ds(cols - reach, reach), :], near1),
        ((0, 1), tr_ref.at[0, pl.ds(cols - 16, 16), :], near0),
        ((0, -1), tr_ref.at[:, pl.ds(0, 16), :], far),
    ]
    for r in (1, -1):
        side = 0 if r == 1 else 1
        for c in (0, 1, -1):
            plan.append(((r, c), edge_ref.at[1 - side], lines.at[side, 1 - c]))
    copies = []
    for k, (step, source, target) in enumerate(plan):
        copy = pltpu.make_async_remote_copy(
            src_ref=source,
            dst_ref=target,
            send_sem=send_sem.at[k],
            recv_sem=recv_sem.at[k],
            device_id=device(step),
            device_id_type=MESH,
        )
        copies.append((step, copy))

        @pl.when(exists(step))
        def _(copy=copy):
            copy.start()

        @pl.when(jnp.logical_not(exists((-step[0], -step[1]))))
        def _(target=target):
            target[...] = jnp.zeros(target.shape, target.dtype)

    spread_at = lax.broadcasted_iota(jnp.int32, (groups * per, lanes), 1) % groups * per
    spread_from = lax.broadcasted_iota(jnp.int32, (groups * per, lanes), 0)
    tn = (((0,), (0,)), ((), ()))
    weight = weight_ref[...].astype(jnp.float32)
    q, bias = [], []
    for ch in range(per):
        spread = (spread_from == spread_at + ch).astype(jnp.float32)
        q.append(
            lax.dot_general(weight, spread, tn, preferred_element_type=jnp.float32)
        )
        bias.append(
            jnp.dot(
                bias_in[...], spread,
                precision=lax.Precision.HIGHEST, preferred_element_type=jnp.float32,
            )
        )
    one = (
        lax.broadcasted_iota(jnp.int32, (groups, lanes), 0)
        == lax.broadcasted_iota(jnp.int32, (groups, lanes), 1) % groups
    ).astype(jnp.float32)
    agg = lax.dot_general(
        agg_in[...], one, tn,
        precision=lax.Precision.HIGHEST, preferred_element_type=jnp.float32,
    )

    lane_row = row_of(lax.broadcasted_iota(jnp.int32, (cin, lanes), 1))
    order = list(range(2, rows + 2)) + [0, 1, rows + 2, rows + 3]
    for step_x in range(3):
        for ch in range(per):
            taps = []
            for step_y in range(3):
                base = (step_y * 3 + step_x) * cin
                taps.append(q[ch][base : base + cin, :])
            for pair in range((rows + 4) // 2):
                halves = []
                for line in order[2 * pair : 2 * pair + 2]:
                    value = jnp.zeros((cin, lanes), jnp.float32)
                    for step_y in range(3):
                        value = jnp.where(lane_row == line - step_y, taps[step_y], value)
                    halves.append(value)
                wc[step_x, pair * 2 * cin : (pair + 1) * 2 * cin, ch * lanes : (ch + 1) * lanes] = (
                    jnp.concatenate(halves, axis=0).astype(jnp.bfloat16)
                )
    used = (rows + 4) * cin
    if used < lanes:
        wc[:, used:, :] = jnp.zeros((3, lanes - used, per * lanes), jnp.bfloat16)

    lane = lax.broadcasted_iota(jnp.int32, (rows, lanes), 1)
    off = row_of(lane) - lax.broadcasted_iota(jnp.int32, (rows, lanes), 0)
    group_main = rows * groups
    part_of = skew_of(lane)
    for step_d in range(3):
        for step_x in range(3):
            value = jnp.zeros((rows, lanes), jnp.float32)
            for step_y in range(3):
                k = 9 * step_d + 3 * step_y + step_x
                value = jnp.where(off == step_y, agg[k : k + 1, :], value)
            high = value.astype(jnp.bfloat16)
            low = (value - high.astype(jnp.float32)).astype(jnp.bfloat16)
            at = (step_d * 3 + step_x) * 2 * rows
            for v, value in enumerate((high, low)):
                begin = at + v * rows
                amat[0, begin : begin + rows, :] = value[:, :group_main]
                for ds in range(skew):
                    own = jnp.where(part_of == ds, value.astype(jnp.float32), 0.0)
                    amat[1 + ds, begin : begin + rows, :] = own[:, group_main:].astype(jnp.bfloat16)

    for step, copy in copies:

        @pl.when(exists((-step[0], -step[1])))
        def _(copy=copy):
            copy.wait_recv()

    base = 16 + D
    main = rows * cin
    pt[1, base - reach : base, 0:main] = near1[...].astype(jnp.float32)
    pt[0, base - 16 : base, 0:main] = near0[...].astype(jnp.float32)
    pt[:, base : base + cols, 0:main] = tr_ref[...].astype(jnp.float32)
    pt[:, base + cols : base + cols + 16, 0:main] = far[...].astype(jnp.float32)
    half = 2 * cin
    for image in range(2):
        for place in range(3):
            block = jnp.concatenate(
                [
                    lines[side, place, image * half : (image + 1) * half, :].astype(jnp.float32)
                    for side in range(2)
                ]
                + [jnp.zeros((lanes - main - 2 * half, cols), jnp.float32)],
                axis=0,
            )
            block = block.T
            if place == 0:
                pt[image, base - reach : base, main:] = block[cols - reach :, :]
            elif place == 1:
                pt[image, base : base + cols, main:] = block
            else:
                pt[image, base + cols : base + cols + 16, main:] = block[:16, :]

    def features(image, first, count, store, scale):
        row_ids = left + first - lead + lax.broadcasted_iota(jnp.int32, (count, lanes), 0)
        line = top + row_of(lax.broadcasted_iota(jnp.int32, (count, lanes), 1))
        keep = (row_ids >= 0) & (row_ids < total_cols) & (line >= 0) & (line < total_rows)
        parts = [
            pt[image, 7 + step_x + first : 7 + step_x + first + count, :].astype(jnp.bfloat16)
            for step_x in range(3)
        ]
        for ch in range(per):
            summed = jnp.broadcast_to(bias[ch], (count, lanes))
            total = None
            for step_x in range(3):
                term = jnp.dot(
                    parts[step_x],
                    wc[step_x, :, ch * lanes : (ch + 1) * lanes],
                    preferred_element_type=jnp.float32,
                )
                total = term if total is None else total + term
            summed = total + summed
            feat = jnp.where(summed >= 0, summed, summed * 0.1)
            feat = feat.astype(jnp.bfloat16).astype(jnp.float32)
            feat = jnp.where(keep, feat * scale, 0.0)
            for tile in range(tiles):
                store[ch * tiles + tile, :, :] = feat[:, tile * 128 : (tile + 1) * 128]

    features(0, lead - 8, cols + 16, lf, 1.0 / per)
    features(1, 0, span, rf, 1.0)

    apart = skew_of(lax.broadcasted_iota(jnp.int32, (span, 128), 1) + group_main)
    for ch in range(per):
        raw[ch, 0:8, :] = jnp.zeros((8, 128), jnp.float32)
        value = rf[ch * tiles + 1, :, :]
        raw[ch, 8 : 8 + span, :] = value
        for ds in range(1, skew):
            value = jnp.where(apart == ds, raw[ch, 8 - ds : 8 - ds + span, :], value)
        rf[ch * tiles + 1, :, :] = value

    edges = []
    for at, begin in ((7, lead - D), (8 + cols, lead + cols - D + 1)):
        parts = []
        for tile in range(tiles):
            total = None
            for ch in range(per):
                k = ch * tiles + tile
                term = lf[k, at : at + 1, :] * rf[k, begin : begin + D, :]
                total = term if total is None else total + term
            parts.append(total.astype(jnp.bfloat16))
        edges.append(jnp.concatenate(parts, axis=1))
    edge = jnp.concatenate(edges, axis=0)
    nt = (((1,), (1,)), ((), ()))
    main_a = amat[0]
    side = lax.dot_general(
        jnp.concatenate([main_a, amat[1]], axis=1), edge, nt, preferred_element_type=jnp.float32
    )
    place = lax.broadcasted_iota(jnp.int32, (rows, 2 * D), 1)
    within = jnp.where(place >= D, place - D, place)
    border = None
    for step_d in range(3):
        pick = []
        for step_x in (0, 2):
            at = (step_d * 3 + step_x) * 2 * rows
            pick.append(side[at : at + rows, :] + side[at + rows : at + 2 * rows, :])
        value = jnp.where(place < D, pick[0], pick[1])
        if step_d == 0:
            value = jnp.where(within == D - 1, 0.0, pltpu.roll(value, 2 * D - 1, 1))
        elif step_d == 2:
            value = jnp.where(within == 0, 0.0, pltpu.roll(value, 1, 1))
        border = value if border is None else border + value

    acc[...] = jnp.zeros_like(acc)

    def product(tile, chunk, d):
        total = None
        for ch in range(per):
            k = ch * tiles + tile
            term = (
                lf[k, 8 + chunk * 16 : 24 + chunk * 16, :]
                * rf[k, pl.ds(lead + chunk * 16 - d, 16), :]
            )
            total = term if total is None else total + term
        return total.astype(jnp.bfloat16)

    def band(block, carry):
        d0 = block * 2 * skew
        beside = []
        for p in range(2):
            for chunk in range(cols // 16):
                beside.append(product(1, chunk, d0 + p * skew))
        cost[0, :, group_main:] = jnp.concatenate(beside, axis=0)
        held = {}
        for ds in range(skew):
            for p in range(2):
                for chunk in range(cols // 16):
                    at = p * cols + chunk * 16
                    cost[ds, at : at + 16, :group_main] = product(0, chunk, d0 + p * skew + ds)
            stack = jnp.concatenate([cost[ds, :, :group_main], cost[0, :, group_main:]], axis=1)
            weights = jnp.concatenate([amat[0], amat[1 + ds]], axis=1)
            got = lax.dot_general(weights, stack, nt, preferred_element_type=jnp.float32)
            for step_x in range(3):
                for p in range(2):
                    for step_d in range(3):
                        at = (step_d * 3 + step_x) * 2 * rows
                        columns = slice(p * cols, (p + 1) * cols)
                        value = got[at : at + rows, columns] + got[at + rows : at + 2 * rows, columns]
                        key = (step_x, p, ds + 2 - step_d)
                        held[key] = held[key] + value if key in held else value
                    done = [ds] if ds < skew - 1 else [ds, ds + 1, ds + 2]
                    for o in done:
                        acc[step_x, d0 + p * skew + o, :, :] += held.pop((step_x, p, o))
        return carry

    lax.fori_loop(0, D // (2 * skew), band, 0)

    lane = lax.broadcasted_iota(jnp.int32, (rows, cols), 1)

    def finish(d, best):
        before = jnp.where(
            lane == 0,
            pltpu.roll(border, lax.rem(d + D + 1, 2 * D), 1),
            pltpu.roll(acc[0, d + 1, :, :], 1, 1),
        )
        after = jnp.where(
            lane == cols - 1, pltpu.roll(border, d, 1), pltpu.roll(acc[2, d + 1, :, :], cols - 1, 1)
        )
        value = acc[1, d + 1, :, :] + before + after
        score[d, :, :] = value
        return jnp.maximum(best, value)

    best = lax.fori_loop(0, D, finish, jnp.full((rows, cols), -jnp.inf, jnp.float32), unroll=4)

    def weigh(d, carry):
        total, moment = carry
        weight = jnp.exp(score[d, :, :] - best)
        return total + weight, moment + weight * d.astype(jnp.float32)

    zero = jnp.zeros((rows, cols), jnp.float32)
    total, moment = lax.fori_loop(0, D, weigh, (zero, zero), unroll=4)
    out_ref[...] = moment / total / D

    for step, copy in copies:

        @pl.when(exists(step))
        def _(copy=copy):
            copy.wait_send()


def on_device(images, conv_weight, conv_bias, agg_weight):
    cin, rows, cols = images.shape[1:]
    groups = agg_weight.shape[0]
    per = conv_weight.shape[0] // groups
    main = rows * cin
    lanes = main + 128
    span = cols + D + 16
    reach = -(-(D + 2) // 16) * 16
    pictures = images.astype(jnp.bfloat16).transpose(0, 2, 1, 3)
    tr = pictures.reshape(2, main, cols).transpose(0, 2, 1)
    edges = jnp.stack([pictures[:, :2], pictures[:, rows - 2 :]]).reshape(2, 4 * cin, cols)
    return pl.pallas_call(
        functools.partial(body, (rows, cols, groups, per, cin)),
        out_shape=jax.ShapeDtypeStruct((rows, cols), jnp.float32),
        in_specs=[pl.BlockSpec(memory_space=pltpu.VMEM)] * 5,
        out_specs=pl.BlockSpec(memory_space=pltpu.VMEM),
        scratch_shapes=[
            pltpu.VMEM((2, span + 16, lanes), jnp.float32),
            pltpu.VMEM((3, lanes, per * lanes), jnp.bfloat16),
            pltpu.VMEM((1 + 64 // groups, 18 * rows, 128), jnp.bfloat16),
            pltpu.VMEM((per * (lanes // 128), cols + 16, 128), jnp.float32),
            pltpu.VMEM((per * (lanes // 128), span, 128), jnp.float32),
            pltpu.VMEM((per, span + 8, 128), jnp.float32),
            pltpu.VMEM((64 // groups, 2 * cols, lanes), jnp.bfloat16),
            pltpu.VMEM((3, D + 2, rows, cols), jnp.float32),
            pltpu.VMEM((D, rows, cols), jnp.float32),
            pltpu.VMEM((16, main), jnp.bfloat16),
            pltpu.VMEM((reach, main), jnp.bfloat16),
            pltpu.VMEM((2, 16, main), jnp.bfloat16),
            pltpu.VMEM((2, 3, 4 * cin, cols), jnp.bfloat16),
            pltpu.SemaphoreType.DMA((9,)),
            pltpu.SemaphoreType.DMA((9,)),
        ],
        compiler_params=pltpu.CompilerParams(collective_id=0, has_side_effects=True),
    )(tr, edges, conv_weight, conv_bias[None], agg_weight)


def solution(mesh):
    in_specs = (P("pairs", None, "row", "col"), P(), P(), P())
    out_specs = P(("pairs", "row"), "col")
    return jax.shard_map(
        on_device, mesh=mesh, in_specs=in_specs, out_specs=out_specs, check_vma=False
    )
```

```python
import functools

import jax
import jax.numpy as jnp
from jax import lax
from jax.experimental import pallas as pl
from jax.experimental.pallas import tpu as pltpu
from jax.sharding import PartitionSpec as P

D = 64


MESH = pl.DeviceIdType.MESH
STEPS = ((0, 1), (0, -1), (1, 0), (-1, 0), (1, 1), (1, -1), (-1, 1), (-1, -1))


def body(
    shape, images_ref, weight_ref, bias_in, agg_in, out_ref,
    pt, wc, amat, lf, rf, raw, cost, acc, score, tr_ref, edge_ref, near0, near1, far, lines, send_sem, recv_sem,
):
    rows, cols, groups, per, cin = shape
    lanes = wc.shape[2] // per
    lead = D + 8
    span = rf.shape[1]
    tiles = lanes // 128
    rows_axis, cols_axis = lax.axis_size("row"), lax.axis_size("col")
    my_row, my_col = lax.axis_index("row"), lax.axis_index("col")
    total_rows = rows * rows_axis
    total_cols = cols * cols_axis
    top = my_row * rows - 1
    left = my_col * cols
    reach = near1.shape[0]
    skew = 128 // (2 * groups)

    def row_of(lane):
        beside = jnp.where((lane // groups) % 2 == 0, 0, rows + 1)
        return jnp.where(lane < rows * groups, lane // groups + 1, beside)

    def skew_of(lane):
        return (lane - rows * groups) // (2 * groups)


    def exists(step):
        r, c = my_row + step[0], my_col + step[1]
        return (r >= 0) & (r < rows_axis) & (c >= 0) & (c < cols_axis)

    def device(step):
        return {"row": my_row + step[0], "col": my_col + step[1]}

    main = rows * cin
    for image in range(2):
        flat = images_ref[image].reshape(main, cols)
        tr_ref[image] = flat.T.astype(jnp.bfloat16)
        for side, first in ((0, 0), (1, rows - 2)):
            pair = [images_ref[image, :, first + y, :] for y in range(2)]
            edge_ref[side, image * 2 * cin : (image + 1) * 2 * cin, :] = jnp.concatenate(
                pair, axis=0
            ).astype(jnp.bfloat16)

    barrier = pltpu.get_barrier_semaphore()
    for step in STEPS:

        @pl.when(exists(step))
        def _(step=step):
            pl.semaphore_signal(barrier, inc=1, device_id=device(step), device_id_type=MESH)

    tall = 1 + (my_row > 0).astype(jnp.int32) + (my_row < rows_axis - 1).astype(jnp.int32)
    wide = 1 + (my_col > 0).astype(jnp.int32) + (my_col < cols_axis - 1).astype(jnp.int32)
    pl.semaphore_wait(barrier, tall * wide - 1)

    plan = [
        ((0, 1), tr_ref.at[1, pl.ds(cols - reach, reach), :], near1),
        ((0, 1), tr_ref.at[0, pl.ds(cols - 16, 16), :], near0),
        ((0, -1), tr_ref.at[:, pl.ds(0, 16), :], far),
    ]
    for r in (1, -1):
        side = 0 if r == 1 else 1
        for c in (0, 1, -1):
            plan.append(((r, c), edge_ref.at[1 - side], lines.at[side, 1 - c]))
    copies = []
    for k, (step, source, target) in enumerate(plan):
        copy = pltpu.make_async_remote_copy(
            src_ref=source,
            dst_ref=target,
            send_sem=send_sem.at[k],
            recv_sem=recv_sem.at[k],
            device_id=device(step),
            device_id_type=MESH,
        )
        copies.append((step, copy))

        @pl.when(exists(step))
        def _(copy=copy):
            copy.start()

        @pl.when(jnp.logical_not(exists((-step[0], -step[1]))))
        def _(target=target):
            target[...] = jnp.zeros(target.shape, target.dtype)

    spread_at = lax.broadcasted_iota(jnp.int32, (groups * per, lanes), 1) % groups * per
    spread_from = lax.broadcasted_iota(jnp.int32, (groups * per, lanes), 0)
    tn = (((0,), (0,)), ((), ()))
    weight = weight_ref[...].astype(jnp.float32)
    q, bias = [], []
    for ch in range(per):
        spread = (spread_from == spread_at + ch).astype(jnp.float32)
        q.append(
            lax.dot_general(weight, spread, tn, preferred_element_type=jnp.float32)
        )
        bias.append(
            jnp.dot(
                bias_in[...], spread,
                precision=lax.Precision.HIGHEST, preferred_element_type=jnp.float32,
            )
        )
    one = (
        lax.broadcasted_iota(jnp.int32, (groups, lanes), 0)
        == lax.broadcasted_iota(jnp.int32, (groups, lanes), 1) % groups
    ).astype(jnp.float32)
    agg = lax.dot_general(
        agg_in[...], one, tn,
        precision=lax.Precision.HIGHEST, preferred_element_type=jnp.float32,
    )

    lane_row = row_of(lax.broadcasted_iota(jnp.int32, (rows, lanes), 1))
    line_off = lane_row - lax.broadcasted_iota(jnp.int32, (rows, lanes), 0)
    near_row = lane_row[:cin]
    for step_x in range(3):
        for ch in range(per):
            columns = slice(ch * lanes, (ch + 1) * lanes)
            taps = []
            for step_y in range(3):
                base = (step_y * 3 + step_x) * cin
                taps.append(q[ch][base : base + cin, :])
            for c in range(cin):
                value = jnp.zeros((rows, lanes), jnp.float32)
                for step_y in range(3):
                    value = jnp.where(line_off == 2 - step_y, taps[step_y][c : c + 1, :], value)
                wc[step_x, c * rows : (c + 1) * rows, columns] = value.astype(jnp.bfloat16)
            for pair in range(2):
                halves = []
                for line in ((0, 1), (rows + 2, rows + 3))[pair]:
                    value = jnp.zeros((cin, lanes), jnp.float32)
                    for step_y in range(3):
                        value = jnp.where(near_row == line - step_y, taps[step_y], value)
                    halves.append(value)
                begin = main + pair * 2 * cin
                wc[step_x, begin : begin + 2 * cin, columns] = (
                    jnp.concatenate(halves, axis=0).astype(jnp.bfloat16)
                )
    used = (rows + 4) * cin
    if used < lanes:
        wc[:, used:, :] = jnp.zeros((3, lanes - used, per * lanes), jnp.bfloat16)

    lane = lax.broadcasted_iota(jnp.int32, (rows, lanes), 1)
    off = row_of(lane) - lax.broadcasted_iota(jnp.int32, (rows, lanes), 0)
    group_main = rows * groups
    part_of = skew_of(lane)
    for step_d in range(3):
        for step_x in range(3):
            value = jnp.zeros((rows, lanes), jnp.float32)
            for step_y in range(3):
                k = 9 * step_d + 3 * step_y + step_x
                value = jnp.where(off == step_y, agg[k : k + 1, :], value)
            high = value.astype(jnp.bfloat16)
            low = (value - high.astype(jnp.float32)).astype(jnp.bfloat16)
            at = (step_d * 3 + step_x) * 2 * rows
            for v, value in enumerate((high, low)):
                begin = at + v * rows
                amat[0, begin : begin + rows, :] = value[:, :group_main]
                for ds in range(skew):
                    own = jnp.where(part_of == ds, value.astype(jnp.float32), 0.0)
                    amat[1 + ds, begin : begin + rows, :] = own[:, group_main:].astype(jnp.bfloat16)

    for step, copy in copies:

        @pl.when(exists((-step[0], -step[1])))
        def _(copy=copy):
            copy.wait_recv()

    base = 16 + D
    pt[1, base - reach : base, 0:main] = near1[...].astype(jnp.float32)
    pt[0, base - 16 : base, 0:main] = near0[...].astype(jnp.float32)
    pt[:, base : base + cols, 0:main] = tr_ref[...].astype(jnp.float32)
    pt[:, base + cols : base + cols + 16, 0:main] = far[...].astype(jnp.float32)
    half = 2 * cin
    for image in range(2):
        for place in range(3):
            block = jnp.concatenate(
                [
                    lines[side, place, image * half : (image + 1) * half, :].astype(jnp.float32)
                    for side in range(2)
                ]
                + [jnp.zeros((lanes - main - 2 * half, cols), jnp.float32)],
                axis=0,
            )
            block = block.T
            if place == 0:
                pt[image, base - reach : base, main:] = block[cols - reach :, :]
            elif place == 1:
                pt[image, base : base + cols, main:] = block
            else:
                pt[image, base + cols : base + cols + 16, main:] = block[:16, :]

    def features(image, first, count, store, scale):
        row_ids = left + first - lead + lax.broadcasted_iota(jnp.int32, (count, lanes), 0)
        line = top + row_of(lax.broadcasted_iota(jnp.int32, (count, lanes), 1))
        keep = (row_ids >= 0) & (row_ids < total_cols) & (line >= 0) & (line < total_rows)
        parts = [
            pt[image, 7 + step_x + first : 7 + step_x + first + count, :].astype(jnp.bfloat16)
            for step_x in range(3)
        ]
        for ch in range(per):
            summed = jnp.broadcast_to(bias[ch], (count, lanes))
            total = None
            for step_x in range(3):
                term = jnp.dot(
                    parts[step_x],
                    wc[step_x, :, ch * lanes : (ch + 1) * lanes],
                    preferred_element_type=jnp.float32,
                )
                total = term if total is None else total + term
            summed = total + summed
            feat = jnp.where(summed >= 0, summed, summed * 0.1)
            feat = feat.astype(jnp.bfloat16).astype(jnp.float32)
            feat = jnp.where(keep, feat * scale, 0.0)
            for tile in range(tiles):
                store[ch * tiles + tile, :, :] = feat[:, tile * 128 : (tile + 1) * 128]

    features(0, lead - 8, cols + 16, lf, 1.0 / per)
    features(1, 0, span, rf, 1.0)

    apart = skew_of(lax.broadcasted_iota(jnp.int32, (span, 128), 1) + group_main)
    for ch in range(per):
        raw[ch, 0:8, :] = jnp.zeros((8, 128), jnp.float32)
        value = rf[ch * tiles + 1, :, :]
        raw[ch, 8 : 8 + span, :] = value
        for ds in range(1, skew):
            value = jnp.where(apart == ds, raw[ch, 8 - ds : 8 - ds + span, :], value)
        rf[ch * tiles + 1, :, :] = value

    edges = []
    for at, begin in ((7, lead - D), (8 + cols, lead + cols - D + 1)):
        parts = []
        for tile in range(tiles):
            total = None
            for ch in range(per):
                k = ch * tiles + tile
                term = lf[k, at : at + 1, :] * rf[k, begin : begin + D, :]
                total = term if total is None else total + term
            parts.append(total.astype(jnp.bfloat16))
        edges.append(jnp.concatenate(parts, axis=1))
    edge = jnp.concatenate(edges, axis=0)
    nt = (((1,), (1,)), ((), ()))
    main_a = amat[0]
    side = lax.dot_general(
        jnp.concatenate([main_a, amat[1]], axis=1), edge, nt, preferred_element_type=jnp.float32
    )
    place = lax.broadcasted_iota(jnp.int32, (rows, 2 * D), 1)
    within = jnp.where(place >= D, place - D, place)
    border = None
    for step_d in range(3):
        pick = []
        for step_x in (0, 2):
            at = (step_d * 3 + step_x) * 2 * rows
            pick.append(side[at : at + rows, :] + side[at + rows : at + 2 * rows, :])
        value = jnp.where(place < D, pick[0], pick[1])
        if step_d == 0:
            value = jnp.where(within == D - 1, 0.0, pltpu.roll(value, 2 * D - 1, 1))
        elif step_d == 2:
            value = jnp.where(within == 0, 0.0, pltpu.roll(value, 1, 1))
        border = value if border is None else border + value

    acc[...] = jnp.zeros_like(acc)

    def product(tile, chunk, d):
        total = None
        for ch in range(per):
            k = ch * tiles + tile
            term = (
                lf[k, 8 + chunk * 16 : 24 + chunk * 16, :]
                * rf[k, pl.ds(lead + chunk * 16 - d, 16), :]
            )
            total = term if total is None else total + term
        return total.astype(jnp.bfloat16)

    def band(block, carry):
        d0 = block * 2 * skew
        beside = []
        for p in range(2):
            for chunk in range(cols // 16):
                beside.append(product(1, chunk, d0 + p * skew))
        cost[0, :, group_main:] = jnp.concatenate(beside, axis=0)
        held = {}
        for ds in range(skew):
            for p in range(2):
                for chunk in range(cols // 16):
                    at = p * cols + chunk * 16
                    cost[ds, at : at + 16, :group_main] = product(0, chunk, d0 + p * skew + ds)
            stack = jnp.concatenate([cost[ds, :, :group_main], cost[0, :, group_main:]], axis=1)
            weights = jnp.concatenate([amat[0], amat[1 + ds]], axis=1)
            got = lax.dot_general(weights, stack, nt, preferred_element_type=jnp.float32)
            for step_x in range(3):
                for p in range(2):
                    for step_d in range(3):
                        at = (step_d * 3 + step_x) * 2 * rows
                        columns = slice(p * cols, (p + 1) * cols)
                        value = got[at : at + rows, columns] + got[at + rows : at + 2 * rows, columns]
                        key = (step_x, p, ds + 2 - step_d)
                        held[key] = held[key] + value if key in held else value
                    done = [ds] if ds < skew - 1 else [ds, ds + 1, ds + 2]
                    for o in done:
                        acc[step_x, d0 + p * skew + o, :, :] += held.pop((step_x, p, o))
        return carry

    lax.fori_loop(0, D // (2 * skew), band, 0)

    lane = lax.broadcasted_iota(jnp.int32, (rows, cols), 1)

    def finish(d, best):
        before = jnp.where(
            lane == 0,
            pltpu.roll(border, lax.rem(d + D + 1, 2 * D), 1),
            pltpu.roll(acc[0, d + 1, :, :], 1, 1),
        )
        after = jnp.where(
            lane == cols - 1, pltpu.roll(border, d, 1), pltpu.roll(acc[2, d + 1, :, :], cols - 1, 1)
        )
        value = acc[1, d + 1, :, :] + before + after
        score[d, :, :] = value
        return jnp.maximum(best, value)

    best = lax.fori_loop(0, D, finish, jnp.full((rows, cols), -jnp.inf, jnp.float32), unroll=16)

    def weigh(d, carry):
        total, moment = carry
        weight = jnp.exp(score[d, :, :] - best)
        return total + weight, moment + weight * d.astype(jnp.float32)

    zero = jnp.zeros((rows, cols), jnp.float32)
    total, moment = lax.fori_loop(0, D, weigh, (zero, zero), unroll=16)
    out_ref[...] = moment / total / D

    for step, copy in copies:

        @pl.when(exists(step))
        def _(copy=copy):
            copy.wait_send()


def on_device(images, conv_weight, conv_bias, agg_weight):
    cin, rows, cols = images.shape[1:]
    groups = agg_weight.shape[0]
    per = conv_weight.shape[0] // groups
    main = rows * cin
    lanes = main + 128
    span = cols + D + 16
    reach = -(-(D + 2) // 16) * 16
    return pl.pallas_call(
        functools.partial(body, (rows, cols, groups, per, cin)),
        out_shape=jax.ShapeDtypeStruct((rows, cols), jnp.float32),
        in_specs=[pl.BlockSpec(memory_space=pltpu.VMEM)] * 4,
        out_specs=pl.BlockSpec(memory_space=pltpu.VMEM),
        scratch_shapes=[
            pltpu.VMEM((2, span + 16, lanes), jnp.float32),
            pltpu.VMEM((3, lanes, per * lanes), jnp.bfloat16),
            pltpu.VMEM((1 + 64 // groups, 18 * rows, 128), jnp.bfloat16),
            pltpu.VMEM((per * (lanes // 128), cols + 16, 128), jnp.float32),
            pltpu.VMEM((per * (lanes // 128), span, 128), jnp.float32),
            pltpu.VMEM((per, span + 8, 128), jnp.float32),
            pltpu.VMEM((64 // groups, 2 * cols, lanes), jnp.bfloat16),
            pltpu.VMEM((3, D + 2, rows, cols), jnp.float32),
            pltpu.VMEM((D, rows, cols), jnp.float32),
            pltpu.VMEM((2, cols, main), jnp.bfloat16),
            pltpu.VMEM((2, 4 * cin, cols), jnp.bfloat16),
            pltpu.VMEM((16, main), jnp.bfloat16),
            pltpu.VMEM((reach, main), jnp.bfloat16),
            pltpu.VMEM((2, 16, main), jnp.bfloat16),
            pltpu.VMEM((2, 3, 4 * cin, cols), jnp.bfloat16),
            pltpu.SemaphoreType.DMA((9,)),
            pltpu.SemaphoreType.DMA((9,)),
        ],
        compiler_params=pltpu.CompilerParams(collective_id=0, has_side_effects=True),
    )(images, conv_weight, conv_bias[None], agg_weight)


def solution(mesh):
    in_specs = (P("pairs", None, "row", "col"), P(), P(), P())
    out_specs = P(("pairs", "row"), "col")
    return jax.shard_map(
        on_device, mesh=mesh, in_specs=in_specs, out_specs=out_specs, check_vma=False
    )
```

```python
import functools

import jax
import jax.numpy as jnp
from jax import lax
from jax.experimental import pallas as pl
from jax.experimental.pallas import tpu as pltpu
from jax.sharding import PartitionSpec as P

D = 64


MESH = pl.DeviceIdType.MESH
STEPS = ((0, 1), (0, -1), (1, 0), (-1, 0), (1, 1), (1, -1), (-1, 1), (-1, -1))


def body(
    shape, images_ref, weight_ref, bias_in, agg_in, out_ref,
    pt, wc, amat, lf, rf, raw, cost, acc, score, tr_ref, edge_ref, near0, near1, far, lines, send_sem, recv_sem,
):
    rows, cols, groups, per, cin = shape
    lanes = wc.shape[2] // per
    lead = D + 8
    span = rf.shape[1]
    tiles = lanes // 128
    rows_axis, cols_axis = lax.axis_size("row"), lax.axis_size("col")
    my_row, my_col = lax.axis_index("row"), lax.axis_index("col")
    total_rows = rows * rows_axis
    total_cols = cols * cols_axis
    top = my_row * rows - 1
    left = my_col * cols
    reach = near1.shape[0]
    skew = 128 // (2 * groups)

    def row_of(lane):
        beside = jnp.where((lane // groups) % 2 == 0, 0, rows + 1)
        return jnp.where(lane < rows * groups, lane // groups + 1, beside)

    def skew_of(lane):
        return (lane - rows * groups) // (2 * groups)


    def exists(step):
        r, c = my_row + step[0], my_col + step[1]
        return (r >= 0) & (r < rows_axis) & (c >= 0) & (c < cols_axis)

    def device(step):
        return {"row": my_row + step[0], "col": my_col + step[1]}

    barrier = pltpu.get_barrier_semaphore()
    for step in STEPS:

        @pl.when(exists(step))
        def _(step=step):
            pl.semaphore_signal(barrier, inc=1, device_id=device(step), device_id_type=MESH)

    main = rows * cin
    for image in range(2):
        flat = images_ref[image].reshape(main, cols)
        tr_ref[image] = flat.T.astype(jnp.bfloat16)
        for side, first in ((0, 0), (1, rows - 2)):
            pair = [images_ref[image, :, first + y, :] for y in range(2)]
            edge_ref[side, image * 2 * cin : (image + 1) * 2 * cin, :] = jnp.concatenate(
                pair, axis=0
            ).astype(jnp.bfloat16)

    spread_at = lax.broadcasted_iota(jnp.int32, (groups * per, lanes), 1) % groups * per
    spread_from = lax.broadcasted_iota(jnp.int32, (groups * per, lanes), 0)
    tn = (((0,), (0,)), ((), ()))
    weight = weight_ref[...].astype(jnp.float32)
    q, bias = [], []
    for ch in range(per):
        spread = (spread_from == spread_at + ch).astype(jnp.float32)
        q.append(
            lax.dot_general(weight, spread, tn, preferred_element_type=jnp.float32)
        )
        bias.append(
            jnp.dot(
                bias_in[...], spread,
                precision=lax.Precision.HIGHEST, preferred_element_type=jnp.float32,
            )
        )
    one = (
        lax.broadcasted_iota(jnp.int32, (groups, lanes), 0)
        == lax.broadcasted_iota(jnp.int32, (groups, lanes), 1) % groups
    ).astype(jnp.float32)
    agg = lax.dot_general(
        agg_in[...], one, tn,
        precision=lax.Precision.HIGHEST, preferred_element_type=jnp.float32,
    )

    lane = lax.broadcasted_iota(jnp.int32, (rows, lanes), 1)
    off = row_of(lane) - lax.broadcasted_iota(jnp.int32, (rows, lanes), 0)
    group_main = rows * groups
    part_of = skew_of(lane)
    for step_d in range(3):
        for step_x in range(3):
            value = jnp.zeros((rows, lanes), jnp.float32)
            for step_y in range(3):
                k = 9 * step_d + 3 * step_y + step_x
                value = jnp.where(off == step_y, agg[k : k + 1, :], value)
            high = value.astype(jnp.bfloat16)
            low = (value - high.astype(jnp.float32)).astype(jnp.bfloat16)
            at = (step_d * 3 + step_x) * 2 * rows
            for v, value in enumerate((high, low)):
                begin = at + v * rows
                amat[0, begin : begin + rows, :] = value[:, :group_main]
                for ds in range(skew):
                    own = jnp.where(part_of == ds, value.astype(jnp.float32), 0.0)
                    amat[1 + ds, begin : begin + rows, :] = own[:, group_main:].astype(jnp.bfloat16)

    tall = 1 + (my_row > 0).astype(jnp.int32) + (my_row < rows_axis - 1).astype(jnp.int32)
    wide = 1 + (my_col > 0).astype(jnp.int32) + (my_col < cols_axis - 1).astype(jnp.int32)
    pl.semaphore_wait(barrier, tall * wide - 1)

    plan = [
        ((0, 1), tr_ref.at[1, pl.ds(cols - reach, reach), :], near1),
        ((0, 1), tr_ref.at[0, pl.ds(cols - 16, 16), :], near0),
        ((0, -1), tr_ref.at[:, pl.ds(0, 16), :], far),
    ]
    for r in (1, -1):
        side = 0 if r == 1 else 1
        for c in (0, 1, -1):
            plan.append(((r, c), edge_ref.at[1 - side], lines.at[side, 1 - c]))
    copies = []
    for k, (step, source, target) in enumerate(plan):
        copy = pltpu.make_async_remote_copy(
            src_ref=source,
            dst_ref=target,
            send_sem=send_sem.at[k],
            recv_sem=recv_sem.at[k],
            device_id=device(step),
            device_id_type=MESH,
        )
        copies.append((step, copy))

        @pl.when(exists(step))
        def _(copy=copy):
            copy.start()

        @pl.when(jnp.logical_not(exists((-step[0], -step[1]))))
        def _(target=target):
            target[...] = jnp.zeros(target.shape, target.dtype)

    lane_row = row_of(lax.broadcasted_iota(jnp.int32, (rows, lanes), 1))
    line_off = lane_row - lax.broadcasted_iota(jnp.int32, (rows, lanes), 0)
    near_row = lane_row[:cin]
    for step_x in range(3):
        for ch in range(per):
            columns = slice(ch * lanes, (ch + 1) * lanes)
            taps = []
            for step_y in range(3):
                base = (step_y * 3 + step_x) * cin
                taps.append(q[ch][base : base + cin, :])
            for c in range(cin):
                value = jnp.zeros((rows, lanes), jnp.float32)
                for step_y in range(3):
                    value = jnp.where(line_off == 2 - step_y, taps[step_y][c : c + 1, :], value)
                wc[step_x, c * rows : (c + 1) * rows, columns] = value.astype(jnp.bfloat16)
            for pair in range(2):
                halves = []
                for line in ((0, 1), (rows + 2, rows + 3))[pair]:
                    value = jnp.zeros((cin, lanes), jnp.float32)
                    for step_y in range(3):
                        value = jnp.where(near_row == line - step_y, taps[step_y], value)
                    halves.append(value)
                begin = main + pair * 2 * cin
                wc[step_x, begin : begin + 2 * cin, columns] = (
                    jnp.concatenate(halves, axis=0).astype(jnp.bfloat16)
                )
    used = (rows + 4) * cin
    if used < lanes:
        wc[:, used:, :] = jnp.zeros((3, lanes - used, per * lanes), jnp.bfloat16)

    acc[...] = jnp.zeros_like(acc)
    base = 16 + D
    pt[:, base : base + cols, 0:main] = tr_ref[...].astype(jnp.float32)

    for step, copy in copies:

        @pl.when(exists((-step[0], -step[1])))
        def _(copy=copy):
            copy.wait_recv()

    base = 16 + D
    pt[1, base - reach : base, 0:main] = near1[...].astype(jnp.float32)
    pt[0, base - 16 : base, 0:main] = near0[...].astype(jnp.float32)
    pt[:, base + cols : base + cols + 16, 0:main] = far[...].astype(jnp.float32)
    half = 2 * cin
    for image in range(2):
        for place in range(3):
            block = jnp.concatenate(
                [
                    lines[side, place, image * half : (image + 1) * half, :].astype(jnp.float32)
                    for side in range(2)
                ]
                + [jnp.zeros((lanes - main - 2 * half, cols), jnp.float32)],
                axis=0,
            )
            block = block.T
            if place == 0:
                pt[image, base - reach : base, main:] = block[cols - reach :, :]
            elif place == 1:
                pt[image, base : base + cols, main:] = block
            else:
                pt[image, base + cols : base + cols + 16, main:] = block[:16, :]

    def features(image, first, count, store, scale):
        row_ids = left + first - lead + lax.broadcasted_iota(jnp.int32, (count, lanes), 0)
        line = top + row_of(lax.broadcasted_iota(jnp.int32, (count, lanes), 1))
        keep = (row_ids >= 0) & (row_ids < total_cols) & (line >= 0) & (line < total_rows)
        parts = [
            pt[image, 7 + step_x + first : 7 + step_x + first + count, :].astype(jnp.bfloat16)
            for step_x in range(3)
        ]
        for ch in range(per):
            summed = jnp.broadcast_to(bias[ch], (count, lanes))
            total = None
            for step_x in range(3):
                term = jnp.dot(
                    parts[step_x],
                    wc[step_x, :, ch * lanes : (ch + 1) * lanes],
                    preferred_element_type=jnp.float32,
                )
                total = term if total is None else total + term
            summed = total + summed
            feat = jnp.where(summed >= 0, summed, summed * 0.1)
            feat = feat.astype(jnp.bfloat16).astype(jnp.float32)
            feat = jnp.where(keep, feat * scale, 0.0)
            for tile in range(tiles):
                store[ch * tiles + tile, :, :] = feat[:, tile * 128 : (tile + 1) * 128]

    features(0, lead - 8, cols + 16, lf, 1.0 / per)
    features(1, 0, span, rf, 1.0)

    apart = skew_of(lax.broadcasted_iota(jnp.int32, (span, 128), 1) + group_main)
    for ch in range(per):
        raw[ch, 0:8, :] = jnp.zeros((8, 128), jnp.float32)
        value = rf[ch * tiles + 1, :, :]
        raw[ch, 8 : 8 + span, :] = value
        for ds in range(1, skew):
            value = jnp.where(apart == ds, raw[ch, 8 - ds : 8 - ds + span, :], value)
        rf[ch * tiles + 1, :, :] = value

    edges = []
    for at, begin in ((7, lead - D), (8 + cols, lead + cols - D + 1)):
        parts = []
        for tile in range(tiles):
            total = None
            for ch in range(per):
                k = ch * tiles + tile
                term = lf[k, at : at + 1, :] * rf[k, begin : begin + D, :]
                total = term if total is None else total + term
            parts.append(total.astype(jnp.bfloat16))
        edges.append(jnp.concatenate(parts, axis=1))
    edge = jnp.concatenate(edges, axis=0)
    nt = (((1,), (1,)), ((), ()))
    main_a = amat[0]
    side = lax.dot_general(
        jnp.concatenate([main_a, amat[1]], axis=1), edge, nt, preferred_element_type=jnp.float32
    )
    place = lax.broadcasted_iota(jnp.int32, (rows, 2 * D), 1)
    within = jnp.where(place >= D, place - D, place)
    border = None
    for step_d in range(3):
        pick = []
        for step_x in (0, 2):
            at = (step_d * 3 + step_x) * 2 * rows
            pick.append(side[at : at + rows, :] + side[at + rows : at + 2 * rows, :])
        value = jnp.where(place < D, pick[0], pick[1])
        if step_d == 0:
            value = jnp.where(within == D - 1, 0.0, pltpu.roll(value, 2 * D - 1, 1))
        elif step_d == 2:
            value = jnp.where(within == 0, 0.0, pltpu.roll(value, 1, 1))
        border = value if border is None else border + value

    def product(tile, chunk, d):
        total = None
        for ch in range(per):
            k = ch * tiles + tile
            term = (
                lf[k, 8 + chunk * 16 : 24 + chunk * 16, :]
                * rf[k, pl.ds(lead + chunk * 16 - d, 16), :]
            )
            total = term if total is None else total + term
        return total.astype(jnp.bfloat16)

    def band(block, carry):
        d0 = block * 2 * skew
        beside = []
        for p in range(2):
            for chunk in range(cols // 16):
                beside.append(product(1, chunk, d0 + p * skew))
        cost[0, :, group_main:] = jnp.concatenate(beside, axis=0)
        held = {}
        for ds in range(skew):
            for p in range(2):
                for chunk in range(cols // 16):
                    at = p * cols + chunk * 16
                    cost[ds, at : at + 16, :group_main] = product(0, chunk, d0 + p * skew + ds)
            stack = jnp.concatenate([cost[ds, :, :group_main], cost[0, :, group_main:]], axis=1)
            weights = jnp.concatenate([amat[0], amat[1 + ds]], axis=1)
            got = lax.dot_general(weights, stack, nt, preferred_element_type=jnp.float32)
            for step_x in range(3):
                for p in range(2):
                    for step_d in range(3):
                        at = (step_d * 3 + step_x) * 2 * rows
                        columns = slice(p * cols, (p + 1) * cols)
                        value = got[at : at + rows, columns] + got[at + rows : at + 2 * rows, columns]
                        key = (step_x, p, ds + 2 - step_d)
                        held[key] = held[key] + value if key in held else value
                    done = [ds] if ds < skew - 1 else [ds, ds + 1, ds + 2]
                    for o in done:
                        acc[step_x, d0 + p * skew + o, :, :] += held.pop((step_x, p, o))
        return carry

    lax.fori_loop(0, D // (2 * skew), band, 0)

    lane = lax.broadcasted_iota(jnp.int32, (rows, cols), 1)

    def finish(d, best):
        before = jnp.where(
            lane == 0,
            pltpu.roll(border, lax.rem(d + D + 1, 2 * D), 1),
            pltpu.roll(acc[0, d + 1, :, :], 1, 1),
        )
        after = jnp.where(
            lane == cols - 1, pltpu.roll(border, d, 1), pltpu.roll(acc[2, d + 1, :, :], cols - 1, 1)
        )
        value = acc[1, d + 1, :, :] + before + after
        score[d, :, :] = value
        return jnp.maximum(best, value)

    best = lax.fori_loop(0, D, finish, jnp.full((rows, cols), -jnp.inf, jnp.float32), unroll=16)

    def weigh(d, carry):
        total, moment = carry
        weight = jnp.exp(score[d, :, :] - best)
        return total + weight, moment + weight * d.astype(jnp.float32)

    zero = jnp.zeros((rows, cols), jnp.float32)
    total, moment = lax.fori_loop(0, D, weigh, (zero, zero), unroll=16)
    out_ref[...] = moment / total / D

    for step, copy in copies:

        @pl.when(exists(step))
        def _(copy=copy):
            copy.wait_send()


def on_device(images, conv_weight, conv_bias, agg_weight):
    cin, rows, cols = images.shape[1:]
    groups = agg_weight.shape[0]
    per = conv_weight.shape[0] // groups
    main = rows * cin
    lanes = main + 128
    span = cols + D + 16
    reach = -(-(D + 2) // 16) * 16
    return pl.pallas_call(
        functools.partial(body, (rows, cols, groups, per, cin)),
        out_shape=jax.ShapeDtypeStruct((rows, cols), jnp.float32),
        in_specs=[pl.BlockSpec(memory_space=pltpu.VMEM)] * 4,
        out_specs=pl.BlockSpec(memory_space=pltpu.VMEM),
        scratch_shapes=[
            pltpu.VMEM((2, span + 16, lanes), jnp.float32),
            pltpu.VMEM((3, lanes, per * lanes), jnp.bfloat16),
            pltpu.VMEM((1 + 64 // groups, 18 * rows, 128), jnp.bfloat16),
            pltpu.VMEM((per * (lanes // 128), cols + 16, 128), jnp.float32),
            pltpu.VMEM((per * (lanes // 128), span, 128), jnp.float32),
            pltpu.VMEM((per, span + 8, 128), jnp.float32),
            pltpu.VMEM((64 // groups, 2 * cols, lanes), jnp.bfloat16),
            pltpu.VMEM((3, D + 2, rows, cols), jnp.float32),
            pltpu.VMEM((D, rows, cols), jnp.float32),
            pltpu.VMEM((2, cols, main), jnp.bfloat16),
            pltpu.VMEM((2, 4 * cin, cols), jnp.bfloat16),
            pltpu.VMEM((16, main), jnp.bfloat16),
            pltpu.VMEM((reach, main), jnp.bfloat16),
            pltpu.VMEM((2, 16, main), jnp.bfloat16),
            pltpu.VMEM((2, 3, 4 * cin, cols), jnp.bfloat16),
            pltpu.SemaphoreType.DMA((9,)),
            pltpu.SemaphoreType.DMA((9,)),
        ],
        compiler_params=pltpu.CompilerParams(collective_id=0, has_side_effects=True),
    )(images, conv_weight, conv_bias[None], agg_weight)


def solution(mesh):
    in_specs = (P("pairs", None, "row", "col"), P(), P(), P())
    out_specs = P(("pairs", "row"), "col")
    return jax.shard_map(
        on_device, mesh=mesh, in_specs=in_specs, out_specs=out_specs, check_vma=False
    )
```

```python
import functools

import jax
import jax.numpy as jnp
from jax import lax
from jax.experimental import pallas as pl
from jax.experimental.pallas import tpu as pltpu
from jax.sharding import PartitionSpec as P

D = 64


MESH = pl.DeviceIdType.MESH
STEPS = ((0, 1), (0, -1), (1, 0), (-1, 0), (1, 1), (1, -1), (-1, 1), (-1, -1))


def body(
    shape, images_ref, weight_ref, bias_in, agg_in, out_ref,
    pt, wc, amat, lf, rf, raw, cost, acc, score, tr_ref, edge_ref, near0, near1, far, lines, send_sem, recv_sem,
):
    rows, cols, groups, per, cin = shape
    lanes = wc.shape[2] // per
    lead = D + 8
    span = rf.shape[1]
    tiles = lanes // 128
    rows_axis, cols_axis = lax.axis_size("row"), lax.axis_size("col")
    my_row, my_col = lax.axis_index("row"), lax.axis_index("col")
    total_rows = rows * rows_axis
    total_cols = cols * cols_axis
    top = my_row * rows - 1
    left = my_col * cols
    reach = near1.shape[0]
    skew = 128 // (2 * groups)

    def row_of(lane):
        beside = jnp.where((lane // groups) % 2 == 0, 0, rows + 1)
        return jnp.where(lane < rows * groups, lane // groups + 1, beside)

    def skew_of(lane):
        return (lane - rows * groups) // (2 * groups)


    def exists(step):
        r, c = my_row + step[0], my_col + step[1]
        return (r >= 0) & (r < rows_axis) & (c >= 0) & (c < cols_axis)

    def device(step):
        return {"row": my_row + step[0], "col": my_col + step[1]}

    barrier = pltpu.get_barrier_semaphore()
    for step in STEPS:

        @pl.when(exists(step))
        def _(step=step):
            pl.semaphore_signal(barrier, inc=1, device_id=device(step), device_id_type=MESH)

    main = rows * cin
    for image in range(2):
        flat = images_ref[image].reshape(main, cols)
        tr_ref[image] = flat.T.astype(jnp.bfloat16)
        for side, first in ((0, 0), (1, rows - 2)):
            pair = [images_ref[image, :, first + y, :] for y in range(2)]
            edge_ref[side, image * 2 * cin : (image + 1) * 2 * cin, :] = jnp.concatenate(
                pair, axis=0
            ).astype(jnp.bfloat16)

    spread_at = lax.broadcasted_iota(jnp.int32, (groups * per, lanes), 1) % groups * per
    spread_from = lax.broadcasted_iota(jnp.int32, (groups * per, lanes), 0)
    tn = (((0,), (0,)), ((), ()))
    weight = weight_ref[...].astype(jnp.float32)
    q, bias = [], []
    for ch in range(per):
        spread = (spread_from == spread_at + ch).astype(jnp.float32)
        q.append(
            lax.dot_general(weight, spread, tn, preferred_element_type=jnp.float32)
        )
        bias.append(
            jnp.dot(
                bias_in[...], spread,
                precision=lax.Precision.HIGHEST, preferred_element_type=jnp.float32,
            )
        )
    one = (
        lax.broadcasted_iota(jnp.int32, (groups, lanes), 0)
        == lax.broadcasted_iota(jnp.int32, (groups, lanes), 1) % groups
    ).astype(jnp.float32)
    agg = lax.dot_general(
        agg_in[...], one, tn,
        precision=lax.Precision.HIGHEST, preferred_element_type=jnp.float32,
    )

    lane = lax.broadcasted_iota(jnp.int32, (rows, lanes), 1)
    off = row_of(lane) - lax.broadcasted_iota(jnp.int32, (rows, lanes), 0)
    group_main = rows * groups
    part_of = skew_of(lane)
    for step_d in range(3):
        for step_x in range(3):
            value = jnp.zeros((rows, lanes), jnp.float32)
            for step_y in range(3):
                k = 9 * step_d + 3 * step_y + step_x
                value = jnp.where(off == step_y, agg[k : k + 1, :], value)
            high = value.astype(jnp.bfloat16)
            low = (value - high.astype(jnp.float32)).astype(jnp.bfloat16)
            at = (step_d * 3 + step_x) * 2 * rows
            for v, value in enumerate((high, low)):
                begin = at + v * rows
                amat[0, begin : begin + rows, :] = value[:, :group_main]
                for ds in range(skew):
                    own = jnp.where(part_of == ds, value.astype(jnp.float32), 0.0)
                    amat[1 + ds, begin : begin + rows, :] = own[:, group_main:].astype(jnp.bfloat16)

    tall = 1 + (my_row > 0).astype(jnp.int32) + (my_row < rows_axis - 1).astype(jnp.int32)
    wide = 1 + (my_col > 0).astype(jnp.int32) + (my_col < cols_axis - 1).astype(jnp.int32)
    pl.semaphore_wait(barrier, tall * wide - 1)

    plan = [
        ((0, 1), tr_ref.at[1, pl.ds(cols - reach, reach), :], near1),
        ((0, 1), tr_ref.at[0, pl.ds(cols - 16, 16), :], near0),
        ((0, -1), tr_ref.at[:, pl.ds(0, 16), :], far),
    ]
    for r in (1, -1):
        side = 0 if r == 1 else 1
        for c in (0, 1, -1):
            plan.append(((r, c), edge_ref.at[1 - side], lines.at[side, 1 - c]))
    copies = []
    for k, (step, source, target) in enumerate(plan):
        copy = pltpu.make_async_remote_copy(
            src_ref=source,
            dst_ref=target,
            send_sem=send_sem.at[k],
            recv_sem=recv_sem.at[k],
            device_id=device(step),
            device_id_type=MESH,
        )
        copies.append((step, copy))

        @pl.when(exists(step))
        def _(copy=copy):
            copy.start()

        @pl.when(jnp.logical_not(exists((-step[0], -step[1]))))
        def _(target=target):
            target[...] = jnp.zeros(target.shape, target.dtype)

    lane_row = row_of(lax.broadcasted_iota(jnp.int32, (rows, lanes), 1))
    line_off = lane_row - lax.broadcasted_iota(jnp.int32, (rows, lanes), 0)
    near_row = lane_row[:cin]
    for step_x in range(3):
        for ch in range(per):
            columns = slice(ch * lanes, (ch + 1) * lanes)
            taps = []
            for step_y in range(3):
                base = (step_y * 3 + step_x) * cin
                taps.append(q[ch][base : base + cin, :])
            for c in range(cin):
                value = jnp.zeros((rows, lanes), jnp.float32)
                for step_y in range(3):
                    value = jnp.where(line_off == 2 - step_y, taps[step_y][c : c + 1, :], value)
                wc[step_x, c * rows : (c + 1) * rows, columns] = value.astype(jnp.bfloat16)
            for pair in range(2):
                halves = []
                for line in ((0, 1), (rows + 2, rows + 3))[pair]:
                    value = jnp.zeros((cin, lanes), jnp.float32)
                    for step_y in range(3):
                        value = jnp.where(near_row == line - step_y, taps[step_y], value)
                    halves.append(value)
                begin = main + pair * 2 * cin
                wc[step_x, begin : begin + 2 * cin, columns] = (
                    jnp.concatenate(halves, axis=0).astype(jnp.bfloat16)
                )
    used = (rows + 4) * cin
    if used < lanes:
        wc[:, used:, :] = jnp.zeros((3, lanes - used, per * lanes), jnp.bfloat16)

    acc[...] = jnp.zeros_like(acc)
    base = 16 + D
    pt[:, base : base + cols, 0:main] = tr_ref[...].astype(jnp.float32)

    for step, copy in copies:

        @pl.when(exists((-step[0], -step[1])))
        def _(copy=copy):
            copy.wait_recv()

    base = 16 + D
    pt[1, base - reach : base, 0:main] = near1[...].astype(jnp.float32)
    pt[0, base - 16 : base, 0:main] = near0[...].astype(jnp.float32)
    pt[:, base + cols : base + cols + 16, 0:main] = far[...].astype(jnp.float32)
    half = 2 * cin
    for image in range(2):
        for place in range(3):
            block = jnp.concatenate(
                [
                    lines[side, place, image * half : (image + 1) * half, :].astype(jnp.float32)
                    for side in range(2)
                ]
                + [jnp.zeros((lanes - main - 2 * half, cols), jnp.float32)],
                axis=0,
            )
            block = block.T
            if place == 0:
                pt[image, base - reach : base, main:] = block[cols - reach :, :]
            elif place == 1:
                pt[image, base : base + cols, main:] = block
            else:
                pt[image, base + cols : base + cols + 16, main:] = block[:16, :]

    def features(image, first, count, store, scale):
        row_ids = left + first - lead + lax.broadcasted_iota(jnp.int32, (count, lanes), 0)
        line = top + row_of(lax.broadcasted_iota(jnp.int32, (count, lanes), 1))
        keep = (row_ids >= 0) & (row_ids < total_cols) & (line >= 0) & (line < total_rows)
        parts = [
            pt[image, 7 + step_x + first : 7 + step_x + first + count, :].astype(jnp.bfloat16)
            for step_x in range(3)
        ]
        for ch in range(per):
            summed = jnp.broadcast_to(bias[ch], (count, lanes))
            total = None
            for step_x in range(3):
                term = jnp.dot(
                    parts[step_x],
                    wc[step_x, :, ch * lanes : (ch + 1) * lanes],
                    preferred_element_type=jnp.float32,
                )
                total = term if total is None else total + term
            summed = total + summed
            feat = jnp.where(summed >= 0, summed, summed * 0.1)
            feat = feat.astype(jnp.bfloat16).astype(jnp.float32)
            feat = jnp.where(keep, feat * scale, 0.0)
            for tile in range(tiles):
                store[ch * tiles + tile, :, :] = feat[:, tile * 128 : (tile + 1) * 128]

    features(0, lead - 8, cols + 16, lf, 1.0 / per)
    features(1, 0, span, rf, 1.0)

    apart = skew_of(lax.broadcasted_iota(jnp.int32, (span, 128), 1) + group_main)
    for ch in range(per):
        raw[ch, 0:8, :] = jnp.zeros((8, 128), jnp.float32)
        value = rf[ch * tiles + 1, :, :]
        raw[ch, 8 : 8 + span, :] = value
        for ds in range(1, skew):
            value = jnp.where(apart == ds, raw[ch, 8 - ds : 8 - ds + span, :], value)
        rf[ch * tiles + 1, :, :] = value

    edges = []
    for at, begin in ((7, lead - D), (8 + cols, lead + cols - D + 1)):
        parts = []
        for tile in range(tiles):
            total = None
            for ch in range(per):
                k = ch * tiles + tile
                term = lf[k, at : at + 1, :] * rf[k, begin : begin + D, :]
                total = term if total is None else total + term
            parts.append(total.astype(jnp.bfloat16))
        edges.append(jnp.concatenate(parts, axis=1))
    edge = jnp.concatenate(edges, axis=0)
    nt = (((1,), (1,)), ((), ()))
    main_a = amat[0]
    side = lax.dot_general(
        jnp.concatenate([main_a, amat[1]], axis=1), edge, nt, preferred_element_type=jnp.float32
    )
    place = lax.broadcasted_iota(jnp.int32, (rows, 2 * D), 1)
    within = jnp.where(place >= D, place - D, place)
    border = None
    for step_d in range(3):
        pick = []
        for step_x in (0, 2):
            at = (step_d * 3 + step_x) * 2 * rows
            pick.append(side[at : at + rows, :] + side[at + rows : at + 2 * rows, :])
        value = jnp.where(place < D, pick[0], pick[1])
        if step_d == 0:
            value = jnp.where(within == D - 1, 0.0, pltpu.roll(value, 2 * D - 1, 1))
        elif step_d == 2:
            value = jnp.where(within == 0, 0.0, pltpu.roll(value, 1, 1))
        border = value if border is None else border + value

    def product(tile, chunk, d):
        total = None
        for ch in range(per):
            k = ch * tiles + tile
            term = (
                lf[k, 8 + chunk * 16 : 24 + chunk * 16, :]
                * rf[k, pl.ds(lead + chunk * 16 - d, 16), :]
            )
            total = term if total is None else total + term
        return total.astype(jnp.bfloat16)

    def band(block, carry):
        d0 = block * 2 * skew
        beside = []
        for p in range(2):
            for chunk in range(cols // 16):
                beside.append(product(1, chunk, d0 + p * skew))
        cost[0, :, group_main:] = jnp.concatenate(beside, axis=0)
        held = {}
        for ds in range(skew):
            for p in range(2):
                for chunk in range(cols // 16):
                    at = p * cols + chunk * 16
                    cost[ds, at : at + 16, :group_main] = product(0, chunk, d0 + p * skew + ds)
            stack = jnp.concatenate([cost[ds, :, :group_main], cost[0, :, group_main:]], axis=1)
            weights = jnp.concatenate([amat[0], amat[1 + ds]], axis=1)
            got = lax.dot_general(weights, stack, nt, preferred_element_type=jnp.float32)
            for step_x in range(3):
                for p in range(2):
                    for step_d in range(3):
                        at = (step_d * 3 + step_x) * 2 * rows
                        columns = slice(p * cols, (p + 1) * cols)
                        value = got[at : at + rows, columns] + got[at + rows : at + 2 * rows, columns]
                        key = (step_x, p, ds + 2 - step_d)
                        held[key] = held[key] + value if key in held else value
                    done = [ds] if ds < skew - 1 else [ds, ds + 1, ds + 2]
                    for o in done:
                        acc[step_x, d0 + p * skew + o, :, :] += held.pop((step_x, p, o))
        return carry

    lax.fori_loop(0, D // (2 * skew), band, 0, unroll=2)

    lane = lax.broadcasted_iota(jnp.int32, (rows, cols), 1)

    def finish(d, best):
        before = jnp.where(
            lane == 0,
            pltpu.roll(border, lax.rem(d + D + 1, 2 * D), 1),
            pltpu.roll(acc[0, d + 1, :, :], 1, 1),
        )
        after = jnp.where(
            lane == cols - 1, pltpu.roll(border, d, 1), pltpu.roll(acc[2, d + 1, :, :], cols - 1, 1)
        )
        value = acc[1, d + 1, :, :] + before + after
        score[d, :, :] = value
        return jnp.maximum(best, value)

    best = lax.fori_loop(0, D, finish, jnp.full((rows, cols), -jnp.inf, jnp.float32), unroll=16)

    def weigh(d, carry):
        total, moment = carry
        weight = jnp.exp(score[d, :, :] - best)
        return total + weight, moment + weight * d.astype(jnp.float32)

    zero = jnp.zeros((rows, cols), jnp.float32)
    total, moment = lax.fori_loop(0, D, weigh, (zero, zero), unroll=16)
    out_ref[...] = moment / total / D

    for step, copy in copies:

        @pl.when(exists(step))
        def _(copy=copy):
            copy.wait_send()


def on_device(images, conv_weight, conv_bias, agg_weight):
    cin, rows, cols = images.shape[1:]
    groups = agg_weight.shape[0]
    per = conv_weight.shape[0] // groups
    main = rows * cin
    lanes = main + 128
    span = cols + D + 16
    reach = -(-(D + 2) // 16) * 16
    return pl.pallas_call(
        functools.partial(body, (rows, cols, groups, per, cin)),
        out_shape=jax.ShapeDtypeStruct((rows, cols), jnp.float32),
        in_specs=[pl.BlockSpec(memory_space=pltpu.VMEM)] * 4,
        out_specs=pl.BlockSpec(memory_space=pltpu.VMEM),
        scratch_shapes=[
            pltpu.VMEM((2, span + 16, lanes), jnp.float32),
            pltpu.VMEM((3, lanes, per * lanes), jnp.bfloat16),
            pltpu.VMEM((1 + 64 // groups, 18 * rows, 128), jnp.bfloat16),
            pltpu.VMEM((per * (lanes // 128), cols + 16, 128), jnp.float32),
            pltpu.VMEM((per * (lanes // 128), span, 128), jnp.float32),
            pltpu.VMEM((per, span + 8, 128), jnp.float32),
            pltpu.VMEM((64 // groups, 2 * cols, lanes), jnp.bfloat16),
            pltpu.VMEM((3, D + 2, rows, cols), jnp.float32),
            pltpu.VMEM((D, rows, cols), jnp.float32),
            pltpu.VMEM((2, cols, main), jnp.bfloat16),
            pltpu.VMEM((2, 4 * cin, cols), jnp.bfloat16),
            pltpu.VMEM((16, main), jnp.bfloat16),
            pltpu.VMEM((reach, main), jnp.bfloat16),
            pltpu.VMEM((2, 16, main), jnp.bfloat16),
            pltpu.VMEM((2, 3, 4 * cin, cols), jnp.bfloat16),
            pltpu.SemaphoreType.DMA((9,)),
            pltpu.SemaphoreType.DMA((9,)),
        ],
        compiler_params=pltpu.CompilerParams(collective_id=0, has_side_effects=True),
    )(images, conv_weight, conv_bias[None], agg_weight)


def solution(mesh):
    in_specs = (P("pairs", None, "row", "col"), P(), P(), P())
    out_specs = P(("pairs", "row"), "col")
    return jax.shard_map(
        on_device, mesh=mesh, in_specs=in_specs, out_specs=out_specs, check_vma=False
    )
```
